32 devices in a mesh: segment: 4 (over y, x), vocab: 8 (over z, core).
Axes of the slice: x: 2, y: 2, z: 4, core: 2. Of those that a mesh axis runs over, the one named last changes fastest.
Arguments:
- trunk_out: bfloat16 [160, 7168], P(None, 'vocab'), may hold values from -12 to 12
- embeds: bfloat16 [164, 7168], P(None, 'vocab'), may hold values from -12 to 12
- token_ids: int32 [164], replicated, may hold values from 0 to 8191
- module_weight: bfloat16 [4, 2, 7168, 7168], P('segment', None, 'vocab'), may hold values from -0.046875 to 0.046875
- hidden_gain: bfloat16 [3, 7168], P(None, 'vocab'), may hold values from 0.25 to 1.75
- embed_gain: bfloat16 [3, 7168], P(None, 'vocab'), may hold values from 0.25 to 1.75
- out_gain: bfloat16 [4, 7168], P('segment'), may hold values from 0.25 to 1.75
- head_weight: bfloat16 [7168, 8192], P('segment', 'vocab'), may hold values from -0.21260502 to 0.21260502
Outputs:
- losses: float32 [4, 160], P('segment')
The draws below stay inside these ranges and needn't reach their ends.
All inputs are finite; a program needn't handle non-finite values.
Results may differ from the reference program's by a relative error of at most 0.00095.
Values may be sent and summed in bfloat16 or wider, within the bound.
No kernel may reach another device: no remote copies, remote signals or barrier semaphores. Data moves between devices by JAX's collectives and lax.ppermute only.
A program may use at most 128 MiB of HBM per device.

```python
import math
import jax
import jax.numpy as jnp
from jax import lax

D = 7168
TOK = 160
DEPTH = 3
VOCAB = 8192
N_SEGMENT = 4


def column_ramp():
    return jnp.exp(jnp.linspace(math.log(0.5), math.log(2.0), D)).astype(jnp.float32)


def rough_rows(key, amount):
    entry_key = jax.random.fold_in(key, 3)
    scale_key = jax.random.fold_in(key, 5)
    row_scales = jnp.exp(jax.random.uniform(scale_key, (amount, 1), jnp.float32, 0.0, math.log(10.0))) / 4.0
    entries = jax.random.normal(entry_key, (amount, D), jnp.float32)
    return jnp.clip(entries * column_ramp()[None, :] * row_scales, -12.0, 12.0)


def draw_trunk_out(key, part):
    entries = rough_rows(jax.random.fold_in(key, 11), TOK)
    return entries.astype(jnp.bfloat16)


def draw_embeds(key, part):
    return rough_rows(jax.random.fold_in(key, 17), TOK + N_SEGMENT).astype(jnp.bfloat16)


def draw_head_weight(key, part):
    entry_key = jax.random.fold_in(key, 19)
    scale = 3.0 / math.sqrt(D)
    entries = jnp.clip(jax.random.normal(entry_key, (D, VOCAB), jnp.float32) * scale, -6.0 * scale, 6.0 * scale)
    return entries.astype(jnp.bfloat16)


def plant(values, rng, low, top_value):
    longest = values.shape.index(max(values.shape))
    spots = []
    for shift in (0, 1):
        where = [jax.random.randint(jax.random.fold_in(rng, axis), (), 0, length) for axis, length in enumerate(values.shape)]
        where[longest] = (where[longest] + shift) % values.shape[longest]
        spots.append(tuple(where))
    return values.at[spots[0]].set(low).at[spots[1]].set(top_value)


def steps_of(stream_key, dims, shards, smallest, top_value):
    level = 1.0
    for dim, shards_of in shards:
        draws = jax.random.uniform(jax.random.fold_in(jax.random.fold_in(stream_key, 6), dim), (shards_of,), jnp.float32, smallest / len(shards), top_value / len(shards))
        level = level * jnp.repeat(jnp.exp(draws), dims[dim] // shards_of).reshape((-1,) + (1,) * (len(dims) - 1 - dim))
    return level


def centred(rng, extent, width, most, split=(), kind=jnp.bfloat16):
    gain = steps_of(rng, extent, split, -0.22, 0.18) if split else 1.0
    values = jax.random.normal(rng, extent, jnp.float32) * width * gain
    return jnp.minimum(jnp.maximum(values, -most), most).astype(kind)


def setup_inputs(seed: int = 0) -> dict:
    keys = jax.random.split(jax.random.key(seed), 9)
    return {
        "trunk_out": draw_trunk_out(jax.random.fold_in(keys[8], 71), 0),
        "embeds": draw_embeds(jax.random.fold_in(keys[8], 71), 0),
        "token_ids": plant(jax.random.randint(keys[2], (TOK + N_SEGMENT,), 0, VOCAB), jax.random.fold_in(keys[2], 1), 0, VOCAB - 1).astype(jnp.int32),
        "module_weight": centred(keys[3], (N_SEGMENT, 2, D, D), (2 * D) ** -0.5, 0.046875, ((0, 4), (2, 8))),
        "hidden_gain": jnp.clip(1.0 + 0.15 * jax.random.normal(keys[4], (DEPTH, D), jnp.float32), 0.25, 1.75).astype(jnp.bfloat16),
        "embed_gain": jnp.clip(1.0 + 0.15 * jax.random.normal(keys[5], (DEPTH, D), jnp.float32), 0.25, 1.75).astype(jnp.bfloat16),
        "out_gain": jnp.clip(1.0 + 0.15 * jax.random.normal(keys[6], (N_SEGMENT, D), jnp.float32), 0.25, 1.75).astype(jnp.bfloat16),
        "head_weight": draw_head_weight(jax.random.fold_in(keys[8], 71), 0),
    }


EPSILON = 1e-06

def rms_scaled(values):
    floats = values.astype(jnp.float32)
    return floats * lax.rsqrt(lax.optimization_barrier(jnp.mean(floats * floats, axis=-1, keepdims=True)) + EPSILON)

def reference(trunk_out, embeds, token_ids, module_weight, hidden_gain, embed_gain, out_gain, head_weight):
    hidden = trunk_out
    results = []
    for level in range(N_SEGMENT):
        if level > 0:
            hidden_normed = (rms_scaled(hidden) * hidden_gain[level - 1].astype(jnp.float32)).astype(jnp.bfloat16)
            embed_rows = lax.dynamic_slice_in_dim(embeds, level, TOK, 0)
            embed_normed = (rms_scaled(embed_rows) * embed_gain[level - 1].astype(jnp.float32)).astype(jnp.bfloat16)
            projected = jnp.dot(hidden_normed, module_weight[level, 0], preferred_element_type=jnp.float32)
            projected = projected + jnp.dot(embed_normed, module_weight[level, 1], preferred_element_type=jnp.float32)
            hidden = projected.astype(jnp.bfloat16)
        head_input = (rms_scaled(hidden) * out_gain[level].astype(jnp.float32)).astype(jnp.bfloat16)
        logits = jnp.dot(head_input, head_weight, preferred_element_type=jnp.float32)
        highest = lax.optimization_barrier(jnp.max(logits, axis=1, keepdims=True))
        spread = highest[:, 0] + jnp.log(lax.optimization_barrier(jnp.sum(jnp.exp(logits - highest), axis=1)))
        target = lax.dynamic_slice_in_dim(token_ids, level + 1, TOK, 0).astype(jnp.int32)
        picked = jnp.take_along_axis(logits, target[:, None], axis=1)[:, 0]
        results.append(spread - picked)
    return jnp.stack(results)
```

```python
import jax
import jax.numpy as jnp
from jax import lax
from jax.sharding import PartitionSpec as P

EPSILON = 1e-06
CORES = 2
BOTH = ("segment", "vocab")
WIRE = jnp.float16


class Grid:
    def __init__(self):
        self.sections = lax.axis_size("segment")
        self.shards = lax.axis_size("vocab")
        self.chips = self.shards // CORES
        self.section = lax.axis_index("segment")
        self.shard = lax.axis_index("vocab")
        self.chip = self.shard // CORES
        self.core = self.shard % CORES

    def send(self, block, target, sources=None):
        pairs = []
        for s in range(self.sections) if sources is None else sources:
            for z in range(self.chips):
                for c in range(CORES):
                    ts, tz, tc = target(s, z, c)
                    pairs.append((s * self.shards + z * CORES + c, ts * self.shards + tz * CORES + tc))
        return lax.ppermute(block, BOTH, pairs)

    def swap_core(self, block):
        return self.send(block, lambda s, z, c: (s, z, 1 - c))

    def swap_chip(self, block, d):
        return self.send(block, lambda s, z, c: (s, z ^ d, c))

    def swap_section(self, block, d):
        return self.send(block, lambda s, z, c: (s ^ d, z, c))

    def combine(self, value, merge):
        value = merge(value, self.swap_core(value))
        values = [value] + [self.swap_chip(value, d) for d in range(1, self.chips)]
        while len(values) > 1:
            values = [merge(a, b) for a, b in zip(values[0::2], values[1::2])]
        return values[0]


def merge_softmax(a, b):
    top = jnp.maximum(a[0], b[0])
    total = a[1] * jnp.exp(a[0] - top) + b[1] * jnp.exp(b[0] - top)
    return jnp.stack([top, total, a[2] + b[2]])


def per_device(
    trunk_out, embeds, token_ids, module_weight, hidden_gain, embed_gain, out_gain, head_weight
):
    grid = Grid()
    sections, chips, section, chip, core = grid.sections, grid.chips, grid.section, grid.chip, grid.core
    tokens, width = trunk_out.shape
    whole_width = module_weight.shape[3]
    vocab_width = head_weight.shape[1]
    depth_count = hidden_gain.shape[0]
    add = lambda a, b: a + b

    def squares(rows):
        return jnp.sum(rows * rows, axis=1)

    def scale_of(total):
        return lax.rsqrt(total / whole_width + EPSILON)

    hidden = trunk_out.astype(jnp.float32)
    embed_rows = lax.dynamic_slice_in_dim(embeds, section, tokens, 0).astype(jnp.float32)
    first = grid.combine(jnp.stack([squares(hidden), squares(embed_rows)]), add)
    scale = scale_of(first[0])
    embed_scale = scale_of(first[1])

    module_index = jnp.maximum(section - 1, 0)
    own_embed_gain = lax.dynamic_index_in_dim(embed_gain, module_index, 0, keepdims=False).astype(jnp.float32)
    own_hidden_gain = lax.dynamic_index_in_dim(hidden_gain, module_index, 0, keepdims=False).astype(jnp.float32)
    gain_slice = lax.dynamic_slice_in_dim(out_gain, grid.shard * width, width, 1)
    out_scaling = grid.send(gain_slice, lambda s, z, c: ((s + 1) % sections, z, c))[0].astype(jnp.float32)

    embed_part = (
        jnp.dot(
            (embed_rows * own_embed_gain).astype(jnp.bfloat16),
            module_weight[0, 1],
            preferred_element_type=jnp.float32,
        )
        * embed_scale[:, None]
    )
    for k in range(1, depth_count + 1):
        product = jnp.dot(
            (hidden * own_hidden_gain).astype(jnp.bfloat16),
            module_weight[0, 0],
            preferred_element_type=jnp.float32,
        )
        partial = product * scale[:, None] + embed_part
        blocks = [partial[:, j * width : (j + 1) * width] for j in range(grid.shards)]
        even = jnp.stack(blocks[0::2])
        odd = jnp.stack(blocks[1::2])
        mine = jnp.where(core == 0, even, odd)
        theirs = jnp.where(core == 0, odd, even).astype(WIRE)
        paired = (mine + grid.swap_core(theirs).astype(jnp.float32)).astype(WIRE)
        received = []
        for d in reversed(range(chips)):
            block = lax.dynamic_index_in_dim(paired, chip ^ d, 0, keepdims=False)
            received.append(
                grid.send(block, lambda s, z, c: ((s + 1) % sections, z ^ d, c), sources=(k,))
            )
        total = sum(part.astype(jnp.float32) for part in received)
        total = total.astype(jnp.bfloat16).astype(jnp.float32)
        arrived = section == (k + 1) % sections
        hidden = jnp.where(arrived, total, hidden)
        scale = jnp.where(arrived, scale_of(grid.combine(squares(hidden)[None], add)[0]), scale)

    head_input = (hidden * scale[:, None] * out_scaling).astype(jnp.bfloat16)
    group = chips // sections
    turned = grid.send(head_input, lambda a, z, c: (z // group, a * group + z % group, c))
    spread = jnp.zeros((chips, tokens, width), jnp.bfloat16)
    pieces = [turned] + [grid.swap_chip(turned, d) for d in range(1, chips)]
    for d in range(chips):
        spread = lax.dynamic_update_index_in_dim(spread, pieces[d], chip ^ d, 0)
    other = grid.swap_core(spread)
    even = jnp.where(core == 0, spread, other).reshape(sections, group, tokens, width)
    odd = jnp.where(core == 0, other, spread).reshape(sections, group, tokens, width)
    logits = 0.0
    for r in range(group):
        for c, half in enumerate((even, odd)):
            first_row = (r * CORES + c) * width
            logits = logits + jnp.dot(
                half[:, r].reshape(sections * tokens, width),
                head_weight[first_row : first_row + width],
                preferred_element_type=jnp.float32,
            )
    logits = logits.reshape(sections, tokens, vocab_width)

    def of_depth(values, k):
        return lax.dynamic_index_in_dim(values, (k + 1) % sections, 0, keepdims=False)

    sent = logits.astype(WIRE)
    rows = of_depth(logits, section)
    for d in reversed(range(1, sections)):
        rows = rows + grid.swap_section(of_depth(sent, section ^ d), d).astype(jnp.float32)
    targets = lax.dynamic_slice_in_dim(token_ids, section + 1, tokens, 0) - grid.shard * vocab_width
    column_ids = lax.broadcasted_iota(jnp.int32, (tokens, vocab_width), 1)
    pick = jnp.sum(jnp.where(column_ids == targets[:, None], rows, 0.0), axis=1)
    top = jnp.max(rows, axis=1)
    total = jnp.sum(jnp.exp(rows - top[:, None]), axis=1)
    top, total, pick = grid.combine(jnp.stack([top, total, pick]), merge_softmax)
    return (top + jnp.log(total) - pick)[None, :]


def solution(mesh):
    in_specs = (
        P(None, "vocab"),
        P(None, "vocab"),
        P(),
        P("segment", None, "vocab", None),
        P(None, "vocab"),
        P(None, "vocab"),
        P("segment", None),
        P("segment", "vocab"),
    )
    out_specs = P("segment", None)
    return jax.shard_map(
        per_device, mesh=mesh, in_specs=in_specs, out_specs=out_specs, check_vma=False
    )
```

```python
import jax
import jax.numpy as jnp
from jax import lax
from jax.sharding import PartitionSpec as P


EPSILON = 1e-06
CORES = 2
BOTH = ("segment", "vocab")
WIRE = jnp.float16


class Grid:
    def __init__(self):
        self.sections = lax.axis_size("segment")
        self.shards = lax.axis_size("vocab")
        self.chips = self.shards // CORES
        self.section = lax.axis_index("segment")
        self.shard = lax.axis_index("vocab")
        self.chip = self.shard // CORES
        self.core = self.shard % CORES

    def send(self, block, target, sources=None):
        pairs = []
        for s in range(self.sections) if sources is None else sources:
            for z in range(self.chips):
                for c in range(CORES):
                    ts, tz, tc = target(s, z, c)
                    pairs.append((s * self.shards + z * CORES + c, ts * self.shards + tz * CORES + tc))
        return lax.ppermute(block, BOTH, pairs)

    def swap_core(self, block):
        return self.send(block, lambda s, z, c: (s, z, 1 - c))

    def swap_chip(self, block, d):
        return self.send(block, lambda s, z, c: (s, z ^ d, c))

    def swap_section(self, block, d):
        return self.send(block, lambda s, z, c: (s ^ d, z, c))

    def combine(self, value, merge):
        value = merge(value, self.swap_core(value))
        values = [value]
        for d in range(1, self.chips):
            values.append(self.swap_chip(value, d))
        while len(values) > 1:
            values = [merge(a, b) for a, b in zip(values[0::2], values[1::2])]
        return values[0]


def merge_softmax(a, b):
    top = jnp.maximum(a[0], b[0])
    total = a[1] * jnp.exp(a[0] - top) + b[1] * jnp.exp(b[0] - top)
    return jnp.stack([top, total, a[2] + b[2]])


def per_device(
    trunk_out, embeds, token_ids, module_weight, hidden_gain, embed_gain, out_gain, head_weight
):
    grid = Grid()
    sections, chips, section, chip, core = grid.sections, grid.chips, grid.section, grid.chip, grid.core
    tokens, width = trunk_out.shape
    whole_width = module_weight.shape[3]
    vocab_width = head_weight.shape[1]
    depth_count = hidden_gain.shape[0]
    last = depth_count
    group = chips // sections
    part_rows = tokens // sections
    add = lambda a, b: a + b

    def squares(rows):
        return jnp.sum(rows * rows, axis=1)

    def scale_of(total, count=whole_width):
        return lax.rsqrt(total / count + EPSILON)

    def narrow(values):
        return values.astype(jnp.bfloat16)

    def wide(values):
        return values.astype(jnp.float32)

    def pick_index(values, i):
        return lax.dynamic_index_in_dim(values, i, 0, keepdims=False)

    turned = grid.send(trunk_out, lambda a, z, c: (z // group, a * group + z % group, c))
    hidden = wide(trunk_out)
    embed_rows = wide(lax.dynamic_slice_in_dim(embeds, section, tokens, 0))
    first = grid.combine(jnp.stack([squares(hidden), squares(embed_rows)]), add)
    scale = scale_of(first[0])
    first_scale = scale
    embed_scale = scale_of(first[1])
    module_index = jnp.maximum(section - 1, 0)
    own_embed_gain = wide(pick_index(embed_gain, module_index))
    own_hidden_gain = wide(pick_index(hidden_gain, module_index))
    embed_input = narrow(embed_rows * own_embed_gain)
    span = CORES * width

    def columns_of(half, i):
        weights = lax.dynamic_slice(
            module_weight, (0, half, 0, i * span), (1, 1, module_weight.shape[2], span)
        )
        return weights.reshape(module_weight.shape[2], span)

    def product(rows, half, i):
        return jnp.dot(rows, columns_of(half, i), preferred_element_type=jnp.float32)

    def paired_partial(rows, i, embed_product, apart=False):
        partial = product(rows, 0, i)
        if apart:
            partial = lax.optimization_barrier(partial)
        partial = partial * scale[:, None] + embed_product * embed_scale[:, None]
        even, odd = partial[:, :width], partial[:, width:]
        mine = jnp.where(core == 0, even, odd)
        theirs = jnp.where(core == 0, odd, even).astype(WIRE)
        got = grid.swap_core(theirs)
        return (mine + wide(got)).astype(WIRE)

    def gathered_gain():
        parts = [out_gain]
        for d in range(1, sections):
            parts.append(grid.swap_section(out_gain, d))
        return parts

    def gain_slice(k, start, size):
        out = lax.dynamic_slice_in_dim(gains[0], start, size, 1)
        for d in range(1, sections):
            out = jnp.where((section ^ d) == k, lax.dynamic_slice_in_dim(gains[d], start, size, 1), out)
        return wide(out[0])

    section_start = section * (whole_width // sections)
    section_width = whole_width // sections

    def both_halves(mine):
        other = grid.swap_core(mine)
        even = jnp.where(core == 0, mine, other)
        odd = jnp.where(core == 0, other, mine)
        return [half[r] for r in range(group) for half in (even, odd)]

    def head_product(pieces):
        logits = 0.0
        for i, piece in enumerate(pieces):
            piece_logits = jnp.dot(piece, head_weight[i * width : (i + 1) * width], preferred_element_type=jnp.float32)
            logits = logits + piece_logits
        return logits

    def broadcast_column(block, at):
        holders = range(at * group, (at + 1) * group)
        out = [jnp.where(chip == holder, block, jnp.zeros_like(block)) for holder in holders]
        for d in range(1, chips):
            pairs = [
                (s * grid.shards + z * CORES + c, s * grid.shards + (z ^ d) * CORES + c)
                for s in range(sections)
                for z in holders
                for c in range(CORES)
            ]
            got = lax.ppermute(block, BOTH, pairs)
            for r, holder in enumerate(holders):
                out[r] = jnp.where((chip ^ d) == holder, got, out[r])
        return jnp.stack(out)

    partial_logits = []
    gains = None
    order = [d for pair in zip(reversed(range(chips)), range(chips)) for d in pair][:chips]
    embed_products = {}
    for k in range(1, depth_count):
        received = []
        rows = narrow(hidden * own_hidden_gain)
        for n, d in enumerate(order):
            if k == 1:
                embed_products[d] = lax.optimization_barrier(product(embed_input, 1, chip ^ d))
            paired = paired_partial(rows, chip ^ d, embed_products[d], k > 1 and n == 0)
            received.append(
                grid.send(paired, lambda s, z, c: ((s + 1) % sections, z ^ d, c), sources=(k,))
            )
        if k == 1:
            gains = gathered_gain()
            if group == 1:
                spread = turned[None]
            else:
                spread = jnp.zeros((group, tokens, width), trunk_out.dtype)
                for e in range(group):
                    swapped = turned if e == 0 else grid.swap_chip(turned, e)
                    spread = lax.dynamic_update_index_in_dim(spread, swapped, (chip ^ e) % group, 0)
            pieces = both_halves(spread)
            columns = gain_slice(0, section_start, section_width)
            pieces = [
                narrow(wide(piece) * first_scale[:, None] * columns[i * width : (i + 1) * width])
                for i, piece in enumerate(pieces)
            ]
            partial_logits.append(head_product(pieces))
        total = wide(narrow(sum(wide(part) for part in received)))
        arrived = section == k + 1
        hidden = jnp.where(arrived, total, hidden)
        scale = jnp.where(arrived, scale_of(grid.combine(squares(hidden)[None], add)[0]), scale)
        apart, apart_scale = lax.optimization_barrier((hidden, scale))
        rows = narrow(apart * apart_scale[:, None] * gain_slice(k, grid.shard * width, width))
        at = sections // 2
        hopped = grid.send(
            rows, lambda a, z, c: (z // group, at * group + z % group, c), sources=(k + 1,)
        )
        partial_logits.append(head_product(both_halves(broadcast_column(hopped, at))))

    rows = narrow(hidden * own_hidden_gain)
    part = jnp.zeros((group, tokens, width), WIRE)
    for n, e in enumerate(reversed(range(sections))):
        s = last ^ e
        blocks = []
        for r in range(group):
            i = s * group + r
            embed_product = embed_products[0]
            for d in range(1, chips):
                embed_product = jnp.where((chip ^ d) == i, embed_products[d], embed_product)
            blocks.append(paired_partial(rows, i, embed_product, n + r == 0))
        block = jnp.stack(blocks)
        if s != last:
            block = grid.send(block, lambda a, z, c: (s, z, c), sources=(last,))
        part = jnp.where(section == s, block, part)
    chip_rows = tokens // chips
    part = part.reshape(group, chips, chip_rows, width).transpose(1, 0, 2, 3)
    total = wide(pick_index(part, chip))
    for d in reversed(range(1, chips)):
        got = grid.swap_chip(pick_index(part, chip ^ d), d)
        total = total + wide(got)
    mine = narrow(total)
    spread = jnp.zeros((chips, group, chip_rows, width), jnp.bfloat16)
    spread = lax.dynamic_update_index_in_dim(spread, mine, chip, 0)
    for d in reversed(range(1, chips)):
        got = grid.swap_chip(mine, d)
        spread = lax.dynamic_update_index_in_dim(spread, got, chip ^ d, 0)
    spread = spread.transpose(1, 0, 2, 3).reshape(group, tokens, width)
    pieces = [wide(piece) for piece in both_halves(spread)]
    last_squares = sum(squares(piece) for piece in pieces)
    last_scale = scale_of(last_squares, section_width)
    columns = gain_slice(last, section_start, section_width)
    logits = head_product([narrow(piece * columns[i * width : (i + 1) * width]) for i, piece in enumerate(pieces)])

    def row_part(values, i):
        return lax.dynamic_slice_in_dim(values, i * part_rows, part_rows, 0)

    sent = (logits * last_scale[:, None]).astype(WIRE)
    own_logits = row_part(logits, section)
    square_sum = row_part(last_squares, section)
    gots = []
    for d in reversed(range(1, sections)):
        got_squares = grid.swap_section(row_part(last_squares, section ^ d), d)
        got = grid.swap_section(row_part(sent, section ^ d), d)
        gots.append((got, got_squares))
    for got, got_squares in gots:
        own_logits = own_logits + wide(got) / scale_of(got_squares, section_width)[:, None]
        square_sum = square_sum + got_squares
    own_logits = own_logits * scale_of(square_sum)[:, None]

    early = jnp.stack(partial_logits + [jnp.zeros_like(partial_logits[0])] * (sections - len(partial_logits)))
    sent = early.astype(WIRE)
    rows = pick_index(early, section)
    for d in reversed(range(1, sections)):
        got = grid.swap_section(pick_index(sent, section ^ d), d)
        rows = rows + wide(got)

    def statistics(values, targets):
        column_ids = lax.broadcasted_iota(jnp.int32, values.shape, 1)
        pick = jnp.sum(jnp.where(column_ids == targets[:, None], values, 0.0), axis=1)
        top = jnp.max(values, axis=1)
        total = jnp.sum(jnp.exp(values - top[:, None]), axis=1)
        return jnp.stack([top, total, pick])

    local_ids = token_ids - grid.shard * vocab_width
    early_statistics = statistics(rows, lax.dynamic_slice_in_dim(local_ids, section + 1, tokens, 0))
    late = statistics(
        own_logits, lax.dynamic_slice_in_dim(local_ids, last + 1 + section * part_rows, part_rows, 0)
    )
    late_parts = [
        jnp.where(section == s, late, grid.send(late, lambda a, z, c: (last, z, c), sources=(s,)))
        if s != last
        else late
        for s in range(sections)
    ]
    values = jnp.where(section == last, jnp.concatenate(late_parts, axis=1), early_statistics)
    top, total, pick = grid.combine(values, merge_softmax)
    return (top + jnp.log(total) - pick)[None, :]


def solution(mesh):
    in_specs = (
        P(None, "vocab"),
        P(None, "vocab"),
        P(),
        P("segment", None, "vocab", None),
        P(None, "vocab"),
        P(None, "vocab"),
        P("segment", None),
        P("segment", "vocab"),
    )
    out_specs = P("segment", None)
    return jax.shard_map(per_device, mesh=mesh, in_specs=in_specs, out_specs=out_specs, check_vma=False)
```

```python
import jax
import jax.numpy as jnp
from jax import lax
from jax.sharding import PartitionSpec as P


EPSILON = 1e-06
CORES = 2
BOTH = ("segment", "vocab")
WIRE = jnp.float16


class Grid:
    def __init__(self):
        self.sections = lax.axis_size("segment")
        self.shards = lax.axis_size("vocab")
        self.chips = self.shards // CORES
        self.section = lax.axis_index("segment")
        self.shard = lax.axis_index("vocab")
        self.chip = self.shard // CORES
        self.core = self.shard % CORES

    def send(self, block, target, sources=None):
        pairs = []
        for s in range(self.sections) if sources is None else sources:
            for z in range(self.chips):
                for c in range(CORES):
                    ts, tz, tc = target(s, z, c)
                    pairs.append((s * self.shards + z * CORES + c, ts * self.shards + tz * CORES + tc))
        return lax.ppermute(block, BOTH, pairs)

    def swap_core(self, block):
        return self.send(block, lambda s, z, c: (s, z, 1 - c))

    def swap_chip(self, block, d):
        return self.send(block, lambda s, z, c: (s, z ^ d, c))

    def swap_section(self, block, d):
        return self.send(block, lambda s, z, c: (s ^ d, z, c))

    def combine(self, value, merge):
        value = merge(value, self.swap_core(value))
        values = [value]
        for d in range(1, self.chips):
            values.append(self.swap_chip(value, d))
        while len(values) > 1:
            values = [merge(a, b) for a, b in zip(values[0::2], values[1::2])]
        return values[0]


def merge_softmax(a, b):
    top = jnp.maximum(a[0], b[0])
    total = a[1] * jnp.exp(a[0] - top) + b[1] * jnp.exp(b[0] - top)
    return jnp.stack([top, total, a[2] + b[2]])


def per_device(
    trunk_out, embeds, token_ids, module_weight, hidden_gain, embed_gain, out_gain, head_weight
):
    grid = Grid()
    sections, chips, section, chip, core = grid.sections, grid.chips, grid.section, grid.chip, grid.core
    tokens, width = trunk_out.shape
    whole_width = module_weight.shape[3]
    vocab_width = head_weight.shape[1]
    depth_count = hidden_gain.shape[0]
    last = depth_count
    group = chips // sections
    part_rows = tokens // sections
    add = lambda a, b: a + b

    def squares(rows):
        return jnp.sum(rows * rows, axis=1)

    def scale_of(total, count=whole_width):
        return lax.rsqrt(total / count + EPSILON)

    def narrow(values):
        return values.astype(jnp.bfloat16)

    def wide(values):
        return values.astype(jnp.float32)

    def pick_index(values, i):
        return lax.dynamic_index_in_dim(values, i, 0, keepdims=False)

    turned = grid.send(trunk_out, lambda a, z, c: (z // group, a * group + z % group, c))
    hidden = wide(trunk_out)
    embed_rows = wide(lax.dynamic_slice_in_dim(embeds, section, tokens, 0))
    first = grid.combine(jnp.stack([squares(hidden), squares(embed_rows)]), add)
    scale = scale_of(first[0])
    first_scale = scale
    embed_scale = scale_of(first[1])
    module_index = jnp.maximum(section - 1, 0)
    own_embed_gain = wide(pick_index(embed_gain, module_index))
    own_hidden_gain = wide(pick_index(hidden_gain, module_index))
    embed_input = narrow(embed_rows * own_embed_gain)
    span = CORES * width

    def columns_of(half, i):
        weights = lax.dynamic_slice(
            module_weight, (0, half, 0, i * span), (1, 1, module_weight.shape[2], span)
        )
        return weights.reshape(module_weight.shape[2], span)

    def product(rows, half, i):
        return jnp.dot(rows, columns_of(half, i), preferred_element_type=jnp.float32)

    def hidden_product(rows, i, apart):
        partial = product(rows, 0, i)
        return lax.optimization_barrier(partial) if apart else partial

    def paired(partial):
        even, odd = partial[:, :width], partial[:, width:]
        mine = jnp.where(core == 0, even, odd)
        theirs = jnp.where(core == 0, odd, even).astype(WIRE)
        got = grid.swap_core(theirs)
        return mine + wide(got)

    def gathered_gain():
        parts = [out_gain]
        for d in range(1, sections):
            parts.append(grid.swap_section(out_gain, d))
        return parts

    def gain_slice(k, start, size):
        out = lax.dynamic_slice_in_dim(gains[0], start, size, 1)
        for d in range(1, sections):
            out = jnp.where((section ^ d) == k, lax.dynamic_slice_in_dim(gains[d], start, size, 1), out)
        return wide(out[0])

    section_start = section * (whole_width // sections)
    section_width = whole_width // sections

    def both_halves(mine):
        other = grid.swap_core(mine)
        even = jnp.where(core == 0, mine, other)
        odd = jnp.where(core == 0, other, mine)
        return [half[r] for r in range(group) for half in (even, odd)]

    def head_product(pieces):
        logits = 0.0
        for i, piece in enumerate(pieces):
            piece_logits = jnp.dot(piece, head_weight[i * width : (i + 1) * width], preferred_element_type=jnp.float32)
            logits = logits + piece_logits
        return logits

    def broadcast_column(block, at):
        holders = range(at * group, (at + 1) * group)
        gots = []
        for d in range(1, chips):
            pairs = [
                (s * grid.shards + z * CORES + c, s * grid.shards + (z ^ d) * CORES + c)
                for s in range(sections)
                for z in holders
                for c in range(CORES)
            ]
            got = lax.ppermute(block, BOTH, pairs)
            gots.append(got)
        out = [jnp.where(chip == holder, block, jnp.zeros_like(block)) for holder in holders]
        for d, got in zip(range(1, chips), gots):
            out = [jnp.where((chip ^ d) == holder, got, kept) for holder, kept in zip(holders, out)]
        return jnp.stack(out)

    partial_logits = []
    gains = None
    order = [d for d in reversed(range(chips)) if d % 2] + [d for d in reversed(range(chips)) if d % 2 == 0]
    embed_paired = {}
    first_scale_here = jnp.where(section == 1, scale, 0.0)
    for k in range(1, depth_count):
        received = []
        from_neighbour = {}
        rows = narrow(hidden * own_hidden_gain)
        for n, d in enumerate(order):
            if k == 1:
                embed_product = lax.optimization_barrier(product(embed_input, 1, chip ^ d))
                partial = hidden_product(rows, chip ^ d, False) * first_scale_here[:, None]
                block = paired(partial + embed_product * embed_scale[:, None])
                embed_paired[d] = block
            else:
                partial = hidden_product(rows, chip ^ d, n == 0) * scale[:, None]
                block = paired(partial) + embed_paired[d]
            if d % 2:
                from_neighbour[d - 1] = grid.send(
                    block.astype(WIRE), lambda s, z, c: (s, z ^ 1, c), sources=(k,)
                )
            else:
                block = block + wide(from_neighbour[d])
                received.append(
                    grid.send(
                        block.astype(WIRE), lambda s, z, c: ((s + 1) % sections, z ^ d, c), sources=(k,)
                    )
                )
        if k == 1:
            gains = gathered_gain()
            if group == 1:
                spread = turned[None]
            else:
                spread = jnp.zeros((group, tokens, width), trunk_out.dtype)
                for e in range(group):
                    swapped = turned if e == 0 else grid.swap_chip(turned, e)
                    spread = lax.dynamic_update_index_in_dim(spread, swapped, (chip ^ e) % group, 0)
            pieces = both_halves(spread)
            columns = gain_slice(0, section_start, section_width)
            pieces = [
                narrow(wide(piece) * first_scale[:, None] * columns[i * width : (i + 1) * width])
                for i, piece in enumerate(pieces)
            ]
            partial_logits.append(head_product(pieces))
        total = wide(narrow(sum(wide(part) for part in received)))
        arrived = section == k + 1
        hidden = jnp.where(arrived, total, hidden)
        hidden_squares = squares(hidden)
        scale = jnp.where(arrived, scale_of(grid.combine(hidden_squares[None], add)[0]), scale)
        apart, apart_scale = lax.optimization_barrier((hidden, scale))
        rows = narrow(apart * apart_scale[:, None] * gain_slice(k, grid.shard * width, width))
        at = sections // 2
        hopped = grid.send(
            rows, lambda a, z, c: (z // group, at * group + z % group, c), sources=(k + 1,)
        )
        partial_logits.append(head_product(both_halves(broadcast_column(hopped, at))))

    rows = narrow(hidden * own_hidden_gain)
    part = jnp.zeros((group, tokens, width), WIRE)
    embed_parts = [embed_paired[d] for d in range(chips)]
    for n, e in enumerate(reversed(range(sections))):
        s = last ^ e
        blocks = []
        for r in range(group):
            i = s * group + r
            embed_part = embed_parts[0]
            for d in range(1, chips):
                embed_part = jnp.where((chip ^ d) == i, embed_parts[d], embed_part)
            partial = hidden_product(rows, i, n + r == 0) * scale[:, None]
            blocks.append((paired(partial) + embed_part).astype(WIRE))
        block = jnp.stack(blocks)
        embed_parts, block = lax.optimization_barrier((embed_parts, block))
        if s != last:
            block = grid.send(block, lambda a, z, c: (s, z, c), sources=(last,))
        part = jnp.where(section == s, block, part)
    chip_rows = tokens // chips
    part = part.reshape(group, chips, chip_rows, width).transpose(1, 0, 2, 3)
    total = wide(pick_index(part, chip))
    for d in reversed(range(1, chips)):
        got = grid.swap_chip(pick_index(part, chip ^ d), d)
        total = total + wide(got)
    mine = narrow(total)
    spread = jnp.zeros((chips, group, chip_rows, width), jnp.bfloat16)
    spread = lax.dynamic_update_index_in_dim(spread, mine, chip, 0)
    for d in reversed(range(1, chips)):
        got = grid.swap_chip(mine, d)
        spread = lax.dynamic_update_index_in_dim(spread, got, chip ^ d, 0)
    spread = spread.transpose(1, 0, 2, 3).reshape(group, tokens, width)
    pieces = [wide(piece) for piece in both_halves(spread)]
    last_squares = sum(squares(piece) for piece in pieces)
    root = jnp.sqrt(last_squares / section_width)
    root_high = lax.reduce_precision(root, 5, 10)
    root_low = lax.reduce_precision((root - root_high) * 1024.0, 5, 10)

    def root_scale(high, low):
        value = high + low / 1024.0
        return value * value, lax.rsqrt(value * value + EPSILON)

    mean_square, last_scale = root_scale(root_high, root_low)
    columns = gain_slice(last, section_start, section_width)
    logits = head_product([narrow(piece * columns[i * width : (i + 1) * width]) for i, piece in enumerate(pieces)])

    def row_part(values, i):
        return lax.dynamic_slice_in_dim(values, i * part_rows, part_rows, 0)

    lane = lax.broadcasted_iota(jnp.int32, (tokens, 128), 1)
    extra = jnp.where(lane == 0, root_high[:, None], jnp.where(lane == 1, root_low[:, None], 0.0))
    sent = jnp.concatenate([logits * last_scale[:, None], extra], axis=1).astype(WIRE)
    own_logits = row_part(logits, section)
    square_sum = row_part(mean_square, section)
    gots = []
    for d in reversed(range(1, sections)):
        gots.append(wide(grid.swap_section(row_part(sent, section ^ d), d)))
    for got in gots:
        got_square, got_scale = root_scale(got[:, vocab_width], got[:, vocab_width + 1])
        own_logits = own_logits + got[:, :vocab_width] / got_scale[:, None]
        square_sum = square_sum + got_square
    own_logits = own_logits * scale_of(square_sum, sections)[:, None]

    early = jnp.stack(partial_logits + [jnp.zeros_like(partial_logits[0])] * (sections - len(partial_logits)))
    sent = early.astype(WIRE)
    rows = pick_index(early, section)
    for d in reversed(range(1, sections)):
        got = grid.send(
            pick_index(sent, section ^ d),
            lambda s, z, c: (s ^ d, z, c),
            sources=[s for s in range(sections) if s ^ d != last],
        )
        rows = rows + wide(got)

    def statistics(values, targets):
        column_ids = lax.broadcasted_iota(jnp.int32, values.shape, 1)
        pick = jnp.sum(jnp.where(column_ids == targets[:, None], values, 0.0), axis=1)
        top = jnp.max(values, axis=1)
        total = jnp.sum(jnp.exp(values - top[:, None]), axis=1)
        return jnp.stack([top, total, pick])

    local_ids = token_ids - grid.shard * vocab_width
    early_statistics = statistics(rows, lax.dynamic_slice_in_dim(local_ids, section + 1, tokens, 0))
    late = statistics(
        own_logits, lax.dynamic_slice_in_dim(local_ids, last + 1 + section * part_rows, part_rows, 0)
    )
    late_parts = [
        jnp.where(section == s, late, grid.send(late, lambda a, z, c: (last, z, c), sources=(s,)))
        if s != last
        else late
        for s in range(sections)
    ]
    values = jnp.where(section == last, jnp.concatenate(late_parts, axis=1), early_statistics)
    top, total, pick = grid.combine(values, merge_softmax)
    return (top + jnp.log(total) - pick)[None, :]


def solution(mesh):
    in_specs = (
        P(None, "vocab"),
        P(None, "vocab"),
        P(),
        P("segment", None, "vocab", None),
        P(None, "vocab"),
        P(None, "vocab"),
        P("segment", None),
        P("segment", "vocab"),
    )
    out_specs = P("segment", None)
    return jax.shard_map(per_device, mesh=mesh, in_specs=in_specs, out_specs=out_specs, check_vma=False)
```
